256 devices in a mesh: section: 4 (over z_lo, core), dp: 64 (over x, y, z_hi).
Axes of the slice: x: 4, y: 4, z: 8 (z_hi: 4, z_lo: 2; z = z_hi * 2 + z_lo), core: 2. Of those that a mesh axis runs over, the one named last changes fastest.
Arguments:
- acts: bfloat16 [4, 24576, 4096], P('section', 'dp'), may hold values from -6 to 6
- cotangent: bfloat16 [24576, 4096], P('dp'), may hold values from -6 to 6
- gains: float32 [4, 4096], P('section'), may hold values from 0.1 to 1.9
- value_w: bfloat16 [4, 4096, 1024], P('section', 'dp'), may hold values from -0.09375 to 0.09375
- output_w: bfloat16 [4, 1024, 4096], P('section', None, 'dp'), may hold values from -0.1875 to 0.1875
- d_map: int32 [4, 64], P('section'), may hold values from 0 to 3
- r_map: int32 [4, 16], P('section'), may hold values from 0 to 3
- lengths: int32 [192], P('dp'), may hold values from 32 to 128, as said below
- item_panels: bfloat16 [64, 4, 2, 128, 128], P('dp', 'section'), may hold values from -24 to 24
- owners: int32 [64], replicated, may hold values from 0 to 63, each once
Outputs:
- grad_in: bfloat16 [4, 24576, 4096], P('section', 'dp')
- scores: float32 [192, 64], P('dp')
The draws below stay inside these ranges and needn't reach their ends.
Inputs may be any that keep to these rules, and one draw needn't show every extreme that they name: `lengths`: some document is fully live (128 tokens) in every draw.
All inputs are finite; a program needn't handle non-finite values.
Results may differ from the reference program's by a relative error of at most 0.015.
Values may be sent and summed in bfloat16 or wider, within the bound.
No kernel may reach another device: no remote copies, remote signals or barrier semaphores. Data moves between devices by JAX's collectives and lax.ppermute only.
A program may use at most 128 MiB of HBM per device.

```python
import jax
import jax.numpy as jnp
from jax import lax

D = 4096
R = 1024
BLOCK = 64
DBINS = 2
RBINS = 2
DOC_LEN = 128
ITEM_DEV = 1
TOKENS = 24576
DOCS = 192
ITEMS = 64
DBLOCKS = 64
RBLOCKS = 16
KD = 128
KR = 128
N_SECTION = 4
N_DP = 64


def draw_lengths(key, part):
    drawn = jax.random.randint(key, (DOCS,), DOC_LEN // 4, DOC_LEN + 1, dtype=jnp.int32)
    slots = jnp.arange(DOCS, dtype=jnp.int32)
    drawn = jnp.where(slots == 0, DOC_LEN, drawn)
    return jnp.where(slots == DOCS - 1, DOC_LEN // 4, drawn)


def touch_ends(result, key, least, top_value):
    shape = result.shape
    spot = [jax.random.randint(jax.random.fold_in(key, axis), (), 0, shape[axis]) for axis in range(len(shape))]
    result = result.at[tuple(spot)].set(least)
    longest = shape.index(max(shape))
    spot[longest] = (spot[longest] + 1) % shape[longest]
    return result.at[tuple(spot)].set(top_value)


def block_levels(key, shape, shards, least, top_value):
    gain, own = 1.0, jax.random.fold_in(key, 6)
    for dim, parts in shards:
        draws = jnp.exp(jax.random.uniform(jax.random.fold_in(own, dim), (parts,), jnp.float32, least / len(shards), top_value / len(shards)))
        gain = gain * jnp.repeat(draws, shape[dim] // parts).reshape([-1 if axis == dim else 1 for axis in range(len(shape))])
    return gain


def gaussian(stream_key, shape, spread, most, cuts=(), kind=jnp.bfloat16):
    result = jax.random.normal(stream_key, shape, jnp.float32) * spread
    if len(cuts) > 0:
        result = block_levels(stream_key, shape, cuts, -0.22, 0.18) * result
    return jnp.clip(result, min=-most, max=most).astype(kind)


def setup_inputs(seed: int = 0) -> dict:
    keys = jax.random.split(jax.random.key(seed), 11)
    acts = gaussian(keys[0], (N_SECTION, TOKENS, D), 1.0, 6.0, ((0, 4), (1, 64)))
    cotangent = gaussian(keys[1], (TOKENS, D), 1.0, 6.0, ((0, 64),))
    gains = jnp.clip(1.0 + 0.18 * jax.random.normal(keys[2], (N_SECTION, D), jnp.float32), 0.1, 1.9)
    value_w = gaussian(keys[3], (N_SECTION, D, R), D ** -0.5, 0.09375, ((0, 4), (1, 64)))
    output_w = gaussian(keys[4], (N_SECTION, R, D), R ** -0.5, 0.1875, ((0, 4), (2, 64)))
    d_map = touch_ends(jax.random.randint(keys[5], (N_SECTION, DBLOCKS), 0, 2 * DBINS), jax.random.fold_in(keys[5], 1), 0, (2 * DBINS) - 1).astype(jnp.int32)
    r_map = touch_ends(jax.random.randint(keys[6], (N_SECTION, RBLOCKS), 0, 2 * RBINS), jax.random.fold_in(keys[6], 1), 0, (2 * RBINS) - 1).astype(jnp.int32)
    lengths = draw_lengths(jax.random.fold_in(keys[10], 71), 0)
    item_panels = gaussian(keys[8], (ITEMS, N_SECTION, 2, KD, KR), 4.0, 24.0, ((0, 64), (1, 4)))
    owners = jax.random.permutation(keys[9], N_DP).astype(jnp.int32)
    return dict(acts=acts, cotangent=cotangent, gains=gains, value_w=value_w, output_w=output_w, d_map=d_map, r_map=r_map, lengths=lengths, item_panels=item_panels, owners=owners)


def normalize(inputs, gain_row):
    return inputs * lax.rsqrt(lax.optimization_barrier(jnp.mean(inputs * inputs, axis=-1, keepdims=True)) + 1e-05) * gain_row

def sketch_matrix(codes, bin_count):
    levels = jnp.arange(bin_count, dtype=jnp.int32)
    sign_row = (1 - 2 * (codes // bin_count)).astype(jnp.float32)
    return jnp.where(levels[:, None] == (codes % bin_count)[None, :], sign_row[None, :], jnp.zeros_like(sign_row)[None, :])

def project_rows(values, sketch):
    row_count = values.shape[0]
    block_count = values.shape[1] // BLOCK
    bin_count = sketch.shape[0]
    pieces = values.astype(jnp.float32).reshape(row_count, block_count, BLOCK)
    mapped = jnp.einsum('tbc,kb->tkc', pieces, sketch, precision=lax.Precision.HIGHEST)
    return mapped.reshape(row_count, bin_count * BLOCK) * (block_count / bin_count) ** (-0.5)

def reference(acts, cotangent, gains, value_w, output_w, d_map, r_map, lengths, item_panels, owners):
    positions = jnp.arange(DOC_LEN, dtype=jnp.int32)
    live_mask = (positions[None, :] < lengths[:, None]).reshape(TOKENS, 1)
    current = jnp.where(live_mask, cotangent, jnp.zeros_like(cotangent))
    feature_width = 2 * KD * KR
    ordered = item_panels.reshape(N_DP, ITEM_DEV, N_SECTION, feature_width)[owners].reshape(ITEMS, N_SECTION, feature_width)
    inverse_len = 1.0 / lengths.astype(jnp.float32)
    scores = jnp.zeros((DOCS, ITEMS), jnp.float32)
    outputs = []
    for section in range(N_SECTION - 1, -1, -1):
        inputs = acts[section].astype(jnp.float32)
        gain_row = gains[section]
        hidden = normalize(inputs, gain_row).astype(jnp.bfloat16)
        values = jnp.dot(hidden, value_w[section], preferred_element_type=jnp.float32).astype(jnp.bfloat16)
        dvalues = jnp.dot(current, output_w[section].T, preferred_element_type=jnp.float32).astype(jnp.bfloat16)
        dhidden = jnp.dot(dvalues, value_w[section].T, preferred_element_type=jnp.float32)
        _, pullback = jax.vjp(lambda probe: normalize(probe, gain_row), inputs)
        grad_next = (current.astype(jnp.float32) + pullback(dhidden)[0]).astype(jnp.bfloat16)
        model_sketch = sketch_matrix(d_map[section], DBINS)
        value_sketch = sketch_matrix(r_map[section], RBINS)
        hidden_proj = project_rows(hidden, model_sketch).reshape(DOCS, DOC_LEN, KD)
        dvalue_proj = project_rows(dvalues, value_sketch).reshape(DOCS, DOC_LEN, KR)
        grad_proj = project_rows(current, model_sketch).reshape(DOCS, DOC_LEN, KD)
        value_proj = project_rows(values, value_sketch).reshape(DOCS, DOC_LEN, KR)
        first_feat = jnp.einsum('dtk,dtj->dkj', hidden_proj, dvalue_proj, precision=lax.Precision.HIGHEST)
        second_feat = jnp.einsum('dtk,dtj->dkj', grad_proj, value_proj, precision=lax.Precision.HIGHEST)
        features = jnp.stack([first_feat, second_feat], axis=1) * inverse_len[:, None, None, None]
        features = features.reshape(DOCS, feature_width).astype(jnp.bfloat16)
        scores = scores + jnp.dot(features, ordered[:, section].T, preferred_element_type=jnp.float32)
        outputs.insert(0, grad_next)
        current = grad_next
    return (jnp.stack(outputs), scores * (KD * KR) ** (-0.5))
```

```python
import functools

import jax
import jax.numpy as jnp
from jax import lax
from jax.experimental import pallas as pl
from jax.experimental.pallas import tpu as pltpu
from jax.sharding import PartitionSpec as P

BLOCK = 64
EPS = 1e-05
ANY = pl.BlockSpec(memory_space=pl.ANY)
SMEM = pl.BlockSpec(memory_space=pltpu.SMEM)
VMEM = pl.BlockSpec(memory_space=pltpu.VMEM)
F32 = jnp.float32
BF16 = jnp.bfloat16
TILES = 8


def projection(codes, width):
    row = lax.broadcasted_iota(jnp.int32, (width, 2 * BLOCK), 0)
    col = lax.broadcasted_iota(jnp.int32, (width, 2 * BLOCK), 1)
    code = jnp.broadcast_to(codes[:, None, None], (codes.shape[0], BLOCK, 2 * BLOCK))
    code = code.reshape(width, 2 * BLOCK)
    hit = (row % BLOCK == col % BLOCK) & (code % 2 == col // BLOCK)
    return jnp.where(hit, 1 - 2 * (code // 2), 0).astype(BF16)


def chain_kernel(
    stage, chunk, rows, meta, g_hbm, x_hbm, gain, w_hbm, pm_hbm, qm, grads_in, gp_in, dvp_in,
    send, grads, gp, dvp,
    wo_s, wv_s, g_s, x_s, pm_s, u_s, out_s, acc_s, dv_s, p_s, w_sem, in_sem, out_sem,
):
    shards, depth = wo_s.shape[0], wo_s.shape[2]
    width = shards * wo_s.shape[1]
    per = shards // TILES
    step = width // TILES
    base = chunk * rows

    def weight(kind, dst, t):
        at = pl.ds(pl.multiple_of(t * per, per), per)
        return pltpu.make_async_copy(w_hbm.at[at, kind], dst.at[at], w_sem.at[1 - kind, t])

    def columns(t):
        return pl.ds(pl.multiple_of(t * step, step), step)

    def result(t, i):
        at = columns(t)
        dst = grads.at[pl.ds(base, rows), at] if i == 0 else send.at[:, at]
        return pltpu.make_async_copy(out_s.at[:, at], dst, out_sem.at[i, t])

    def small(i):
        dst = (gp, dvp)[i].at[pl.ds(base, rows)]
        return pltpu.make_async_copy(p_s.at[i], dst, in_sem.at[3 + i])

    results = range(1 if send is None else 2)

    @pl.when(meta[0] == stage)
    def _():
        cg = pltpu.make_async_copy(g_hbm, g_s, in_sem.at[0])
        cx = pltpu.make_async_copy(x_hbm.at[pl.ds(base, rows)], x_s, in_sem.at[1])
        cp = pltpu.make_async_copy(pm_hbm, pm_s, in_sem.at[2])
        cg.start()
        weight(1, wo_s, 0).start()
        cx.start()

        def begin(kind, dst, first):
            @pl.loop(first, TILES)
            def _(t):
                weight(kind, dst, t).start()

        begin(1, wo_s, 1)
        begin(0, wv_s, 0)
        cp.start()
        acc_s[...] = jnp.zeros_like(acc_s)
        cg.wait()

        @pl.loop(0, TILES)
        def _(t):
            weight(1, wo_s, t).wait()
            acc_s[...] += jnp.dot(
                g_s[:, columns(t)],
                wo_s[pl.ds(pl.multiple_of(t * per, per), per)].reshape(step, depth),
                preferred_element_type=F32,
            )

        dv_s[...] = acc_s[...].astype(BF16)
        cx.wait()

        def back(t, sums):
            weight(0, wv_s, t).wait()
            dh = lax.dot_general(
                dv_s[...],
                wv_s[pl.ds(pl.multiple_of(t * per, per), per)].reshape(step, depth),
                (((1,), (1,)), ((), ())),
                preferred_element_type=F32,
            )
            at = columns(t)
            u = dh * gain[:, at]
            x = x_s[:, at].astype(F32)
            u_s[:, at] = u
            return (
                sums[0] + jnp.sum(u * x, axis=-1, keepdims=True),
                sums[1] + jnp.sum(x * x, axis=-1, keepdims=True),
            )

        zero = jnp.zeros((rows, 1), F32)
        total, square = lax.fori_loop(0, TILES, back, (zero, zero))
        r = lax.rsqrt(square * (1.0 / width) + EPS)
        drop = r * r * r * total * (1.0 / width)

        @pl.loop(0, TILES)
        def _(t):
            at = columns(t)
            grad = g_s[:, at].astype(F32) + (r * u_s[:, at] - drop * x_s[:, at].astype(F32))
            out_s[:, at] = grad.astype(BF16)
            for i in results:
                result(t, i).start()

        cp.wait()
        p_s[0] = jnp.dot(g_s[...], pm_s[...], preferred_element_type=F32)
        p_s[1] = jnp.dot(dv_s[...], qm[...], preferred_element_type=F32)
        for i in range(2):
            small(i).start()

        @pl.loop(0, TILES)
        def _(t):
            for i in results:
                result(t, i).wait()

        for i in range(2):
            small(i).wait()


def chain(stage, chunk, meta, g, x, gain, w, pm, qm, state):
    rows, width = g.shape
    shards, _, per_shard, depth = w.shape
    last = stage == 0
    kernel = functools.partial(chain_kernel, stage, chunk, rows)
    if last:
        def kernel(*refs):
            return chain_kernel(stage, chunk, rows, *refs[:10], None, *refs[10:])
    out_shape = [jax.ShapeDtypeStruct(s.shape, s.dtype) for s in state]
    if not last:
        out_shape = [jax.ShapeDtypeStruct((rows, width), BF16)] + out_shape
    off = 0 if last else 1
    outs = pl.pallas_call(
        kernel,
        out_shape=out_shape,
        in_specs=[SMEM, ANY, ANY, VMEM, ANY, ANY, VMEM, ANY, ANY, ANY],
        out_specs=[ANY] * len(out_shape),
        input_output_aliases={7: off, 8: off + 1, 9: off + 2},
        scratch_shapes=[
            pltpu.VMEM((shards, per_shard, depth), BF16),
            pltpu.VMEM((shards, per_shard, depth), BF16),
            pltpu.VMEM((rows, width), BF16),
            pltpu.VMEM((rows, width), BF16),
            pltpu.VMEM(pm.shape, BF16),
            pltpu.VMEM((rows, width), F32),
            pltpu.VMEM((rows, width), BF16),
            pltpu.VMEM((rows, depth), F32),
            pltpu.VMEM((rows, depth), BF16),
            pltpu.VMEM((2, rows, 2 * BLOCK), F32),
            pltpu.SemaphoreType.DMA((2, TILES)),
            pltpu.SemaphoreType.DMA((5,)),
            pltpu.SemaphoreType.DMA((2, TILES)),
        ],
        compiler_params=pltpu.CompilerParams(vmem_limit_bytes=44 << 20),
        cost_estimate=pl.CostEstimate(
            flops=4 * rows * width * depth, bytes_accessed=4 * width * depth, transcendentals=0
        ),
        name=f"chain_{stage}_{chunk}",
    )(meta, g, x, gain, w, pm, qm, *state)
    if last:
        return None, tuple(outs)
    return outs[0], tuple(outs[1:])


def value_kernel(h, w_hbm, qm, after, out, wv_s, acc_s, w_sem):
    shards, depth = wv_s.shape[0], wv_s.shape[2]
    per = shards // TILES
    step = shards * wv_s.shape[1] // TILES

    def weight(t):
        at = pl.ds(pl.multiple_of(t * per, per), per)
        return pltpu.make_async_copy(w_hbm.at[at, 0], wv_s.at[at], w_sem.at[t])

    @pl.loop(0, TILES)
    def _(t):
        weight(t).start()

    acc_s[...] = jnp.zeros_like(acc_s)

    @pl.loop(0, TILES)
    def _(t):
        weight(t).wait()
        acc_s[...] += jnp.dot(
            h[:, pl.ds(pl.multiple_of(t * step, step), step)],
            wv_s[pl.ds(pl.multiple_of(t * per, per), per)].reshape(step, depth),
            preferred_element_type=F32,
        )

    out[...] = jnp.dot(acc_s[...].astype(BF16), qm[...], preferred_element_type=F32)


def value_proj(h, w, qm, after):
    shards, _, per_shard, depth = w.shape
    rows, width = h.shape
    return pl.pallas_call(
        value_kernel,
        out_shape=jax.ShapeDtypeStruct((rows, 2 * BLOCK), F32),
        in_specs=[VMEM, ANY, VMEM, ANY],
        out_specs=VMEM,
        scratch_shapes=[
            pltpu.VMEM((shards, per_shard, depth), BF16),
            pltpu.VMEM((rows, depth), F32),
            pltpu.SemaphoreType.DMA((TILES,)),
        ],
        compiler_params=pltpu.CompilerParams(vmem_limit_bytes=40 << 20),
        cost_estimate=pl.CostEstimate(
            flops=2 * rows * width * depth, bytes_accessed=2 * width * depth, transcendentals=0
        ),
        name="value_proj",
    )(h, w, qm, after)


def score_kernel(docs, scale, owners, lens, hp, vp, gp, dvp, panels, out, feat_s, acc_s):
    slots = hp.shape[0] // docs
    side = hp.shape[1]
    dims = (((0,), (0,)), ((), ()))
    for d in range(docs):
        rows = slice(d * slots, (d + 1) * slots)
        inv = scale / lens[d].astype(F32)
        for i, (a, b) in enumerate(((hp, dvp), (gp, vp))):
            f = lax.dot_general(
                a[rows, :], b[rows, :], dims, precision=lax.Precision.HIGHEST,
                preferred_element_type=F32,
            )
            feat_s[d, i * side : (i + 1) * side, :] = (f * inv).astype(BF16).astype(F32)

    def item(j, carry):
        p = panels[owners[j]].astype(F32)
        for d in range(docs):
            acc_s[d, pl.ds(j, 1), :] = jnp.sum(p * feat_s[d], axis=0, keepdims=True)
        return carry

    lax.fori_loop(0, panels.shape[0], item, 0)
    ones = jnp.ones((8, side), F32)
    for d in range(docs):
        total = lax.dot_general(
            ones, acc_s[d], (((1,), (1,)), ((), ())), precision=lax.Precision.HIGHEST,
            preferred_element_type=F32,
        )
        out[d : d + 1, :] = total[:1] * (1.0 / side)


def score(owners, lens, hp, vp, gp, dvp, panels):
    docs = lens.shape[0]
    items, high, side = panels.shape
    return pl.pallas_call(
        functools.partial(score_kernel, docs, 1.0 / 16),
        out_shape=jax.ShapeDtypeStruct((docs, items), F32),
        in_specs=[SMEM, SMEM] + [VMEM] * 5,
        out_specs=VMEM,
        scratch_shapes=[
            pltpu.VMEM((docs, high, side), F32),
            pltpu.VMEM((docs, items, side), F32),
        ],
        compiler_params=pltpu.CompilerParams(vmem_limit_bytes=32 << 20),
        name="score",
    )(owners, lens, hp, vp, gp, dvp, panels)


def gather_weights(wv, wo):
    w = jnp.stack([wv, wo])[None]
    return lax.all_gather(w, "dp", axis=0, tiled=True)


def body(acts, cotangent, gains, value_w, output_w, d_map, r_map, lengths, item_panels, owners):
    sections = lax.axis_size("section")
    section = lax.axis_index("section")
    x = acts[0]
    tokens, width = x.shape
    docs = lengths.shape[0]
    slots = tokens // docs
    w = gather_weights(value_w[0], output_w[0].T)
    panels = lax.all_gather(item_panels.reshape(1, -1, 2 * BLOCK), "dp", axis=0, tiled=True)

    pm = projection(d_map[0], width)
    qm = projection(r_map[0], value_w.shape[2])
    gain = gains
    xf = x.astype(F32)
    hidden = (xf * lax.rsqrt(jnp.mean(xf * xf, axis=-1, keepdims=True) + EPS) * gain).astype(BF16)
    hp = jnp.dot(hidden, pm, preferred_element_type=F32)
    live = (jnp.arange(slots, dtype=jnp.int32)[None, :] < lengths[:, None]).reshape(docs, slots, 1)
    cot = jnp.where(live, cotangent.reshape(docs, slots, width), 0).astype(BF16)
    meta = section.reshape(1)
    state = (
        jnp.zeros((tokens, width), BF16),
        jnp.zeros((tokens, 2 * BLOCK), F32),
        jnp.zeros((tokens, 2 * BLOCK), F32),
    )
    incoming = [cot[d] for d in range(docs)]
    vp = None
    for stage in range(sections - 1, -1, -1):
        arrived = []
        for d in range(docs):
            send, state = chain(stage, d, meta, incoming[d], x, gain, w, pm, qm, state)
            if stage > 0:
                arrived.append(lax.ppermute(send, "section", [(stage, stage - 1)]))
        incoming = arrived
        if vp is None:
            vp = value_proj(hidden, w, qm, send)
    grads, gp, dvp = state
    part = score(owners, lengths, hp, vp, gp, dvp, panels)
    total = part
    for k in range(1, sections):
        total = total + lax.ppermute(
            part, "section", [(i, (i + k) % sections) for i in range(sections)]
        )
    return (grads[None], total)


def solution(mesh):
    in_specs = (
        P("section", "dp", None),
        P("dp", None),
        P("section", None),
        P("section", "dp", None),
        P("section", None, "dp"),
        P("section", None),
        P("section", None),
        P("dp"),
        P("dp", "section", None, None, None),
        P(),
    )
    out_specs = (P("section", "dp", None), P("dp", None))
    return jax.shard_map(body, mesh=mesh, in_specs=in_specs, out_specs=out_specs, check_vma=False)
```

```python
import functools

import jax
import jax.numpy as jnp
from jax import lax
from jax.experimental import pallas as pl
from jax.experimental.pallas import tpu as pltpu
from jax.sharding import PartitionSpec as P

BLOCK = 64
EPS = 1e-05
ANY = pl.BlockSpec(memory_space=pl.ANY)
SMEM = pl.BlockSpec(memory_space=pltpu.SMEM)
VMEM = pl.BlockSpec(memory_space=pltpu.VMEM)
F32 = jnp.float32
BF16 = jnp.bfloat16
TILES = 4
CHUNKS = 3
SIDE = 4


def prepare_kernel(d_map, r_map, x, gain, pm, qm, hidden, hp, hp_s, sem):
    row = lax.broadcasted_iota(jnp.int32, (BLOCK, 2 * BLOCK), 0)
    col = lax.broadcasted_iota(jnp.int32, (BLOCK, 2 * BLOCK), 1)
    unit = [jnp.where(row + k * BLOCK == col, 1.0, 0.0).astype(F32) for k in range(2)]
    for codes, out in ((d_map, pm), (r_map, qm)):

        @pl.loop(0, codes.shape[1])
        def _(b, codes=codes, out=out):
            code = codes[0, b]
            sign = (1 - 2 * (code // 2)).astype(F32)
            high = (code % 2).astype(F32)
            block = sign * (unit[0] * (1.0 - high) + unit[1] * high)
            out[pl.ds(pl.multiple_of(b * BLOCK, BLOCK), BLOCK), :] = block.astype(BF16)

    part = 128

    @pl.loop(0, x.shape[0] // part)
    def _(i):
        at = pl.ds(pl.multiple_of(i * part, part), part)
        xf = x[at, :].astype(F32)
        r = lax.rsqrt(jnp.mean(xf * xf, axis=-1, keepdims=True) + EPS)
        hidden[at, :] = (xf * r * gain[...]).astype(BF16)
        hp_s[at, :] = jnp.dot(hidden[at, :], pm[...], preferred_element_type=F32)

    copy = pltpu.make_async_copy(hp_s, hp, sem)
    copy.start()
    copy.wait()


def prepare(d_map, r_map, x, gain):
    rows, width = x.shape
    depth = r_map.shape[1] * BLOCK
    side = 2 * BLOCK
    return pl.pallas_call(
        prepare_kernel,
        out_shape=[
            pltpu.VMEM((width, side), BF16),
            pltpu.VMEM((depth, side), BF16),
            jax.ShapeDtypeStruct((rows, width), BF16),
            pltpu.HBM((rows, side), F32),
        ],
        in_specs=[SMEM, SMEM, VMEM, VMEM],
        out_specs=[VMEM] * 3 + [ANY],
        scratch_shapes=[pltpu.VMEM((rows, side), F32), pltpu.SemaphoreType.DMA],
        compiler_params=pltpu.CompilerParams(vmem_limit_bytes=24 << 20),
        cost_estimate=pl.CostEstimate(
            flops=4 * rows * width * side, bytes_accessed=6 * rows * width, transcendentals=0
        ),
        name="prepare",
    )(d_map, r_map, x, gain)


def load_kernel(plan, first, *refs):
    meta = refs[0]
    pieces = refs[1 : 1 + len(plan)]
    n = 1 + len(plan) + (0 if first else 2)
    outs = refs[n : n + 2]
    sem = refs[n + 2]
    me = (meta[1], meta[2], meta[3])

    def place(coord):
        return (coord[0] * SIDE + coord[1]) * SIDE + coord[2]

    def copies(go):
        at = 0
        for ref, (kind, axes, fixed, start) in zip(pieces, plan):
            if kind is None:
                count = ref.shape[0] * 2

                def one(i, ref=ref, at=at):
                    for k in range(2):
                        yield ref.at[i, k], outs[k].at[i * SIDE + me[2]], sem.at[at + 2 * i + k]

                total = ref.shape[0]
            else:
                p, q = axes
                deep = ref.shape[1]
                count = ref.shape[0] * deep

                def one(i, ref=ref, at=at, kind=kind, p=p, q=q, fixed=fixed, start=start, deep=deep):
                    near, far = i // deep, i % deep
                    coord = [None, None, (me[2] + 1 + far) % SIDE]
                    coord[p] = (me[p] + start + near) % SIDE
                    coord[q] = (me[q] + fixed) % SIDE
                    yield ref.at[near, far], outs[kind].at[place(coord)], sem.at[at + i]

                total = count

            @pl.loop(0, total)
            def _(i, one=one):
                for src, dst, sm in one(i):
                    go(pltpu.make_async_copy(src, dst, sm))

            at += count

    copies(lambda c: c.start())
    copies(lambda c: c.wait())


def outside(arrays):
    return [pltpu.with_memory_space_constraint(w, pltpu.HBM) for w in arrays]


def resident(weights):
    return [pltpu.with_memory_space_constraint(w, pltpu.VMEM) for w in weights]


def load(plan, meta, pieces, weights, shape):
    first = weights is None
    count = sum(p.shape[0] * p.shape[1] for p in pieces)
    n = 1 + len(pieces)
    return pl.pallas_call(
        functools.partial(load_kernel, plan, first),
        out_shape=[pltpu.VMEM(shape, BF16)] * 2,
        in_specs=[SMEM] + [ANY] * len(pieces) + ([] if first else [VMEM] * 2),
        out_specs=[VMEM] * 2,
        input_output_aliases={} if first else {n: 0, n + 1: 1},
        scratch_shapes=[pltpu.SemaphoreType.DMA((count,))],
        compiler_params=pltpu.CompilerParams(vmem_limit_bytes=4 << 20),
        cost_estimate=pl.CostEstimate(
            flops=0, bytes_accessed=sum(p.size for p in pieces) * 2, transcendentals=0
        ),
        name="load_first" if first else "load_last",
    )(meta, *outside(pieces), *(() if first else resident(weights)))


def chain_kernel(
    stage, base, meta, g_hbm, x_hbm, gain, wv, wo, pm, qm, send, grads, gp, dvp,
    g_s, x_s, u_s, out_s, acc_s, dv_s, p_s, in_sem, out_sem,
):
    rows, width = g_s.shape
    shards, depth = wo.shape[0], wo.shape[2]
    per = shards // TILES
    step = width // TILES

    def weight(ref, t):
        return ref[pl.ds(pl.multiple_of(t * per, per), per)].reshape(step, depth)

    def columns(t):
        return pl.ds(pl.multiple_of(t * step, step), step)

    def result(t, i):
        at = columns(t)
        dst = grads.at[pl.ds(base, rows), at] if i == 0 else send.at[:, at]
        return pltpu.make_async_copy(out_s.at[:, at], dst, out_sem.at[i, t])

    def small(i):
        dst = (gp, dvp)[i].at[pl.ds(base, rows)]
        return pltpu.make_async_copy(p_s.at[i], dst, in_sem.at[3 + i])

    results = range(1 if send is None else 2)

    @pl.when(meta[0] == stage)
    def _():
        cg = pltpu.make_async_copy(g_hbm, g_s, in_sem.at[0])
        cx = pltpu.make_async_copy(x_hbm.at[pl.ds(base, rows)], x_s, in_sem.at[1])
        cg.start()
        cx.start()
        acc_s[...] = jnp.zeros_like(acc_s)
        cg.wait()

        @pl.loop(0, TILES)
        def _(t):
            acc_s[...] += jnp.dot(g_s[:, columns(t)], weight(wo, t), preferred_element_type=F32)

        dv_s[...] = acc_s[...].astype(BF16)
        cx.wait()

        def back(t, sums):
            dh = lax.dot_general(
                dv_s[...], weight(wv, t), (((1,), (1,)), ((), ())), preferred_element_type=F32
            )
            at = columns(t)
            u = dh * gain[:, at]
            x = x_s[:, at].astype(F32)
            u_s[:, at] = u
            return (
                sums[0] + jnp.sum(u * x, axis=-1, keepdims=True),
                sums[1] + jnp.sum(x * x, axis=-1, keepdims=True),
            )

        zero = jnp.zeros((rows, 1), F32)
        total, square = lax.fori_loop(0, TILES, back, (zero, zero))
        r = lax.rsqrt(square * (1.0 / width) + EPS)
        drop = r * r * r * total * (1.0 / width)

        @pl.loop(0, TILES)
        def _(t):
            at = columns(t)
            grad = g_s[:, at].astype(F32) + (r * u_s[:, at] - drop * x_s[:, at].astype(F32))
            out_s[:, at] = grad.astype(BF16)
            for i in results:
                result(t, i).start()

        p_s[0] = jnp.dot(g_s[...], pm[...], preferred_element_type=F32)
        p_s[1] = jnp.dot(dv_s[...], qm[...], preferred_element_type=F32)
        for i in range(2):
            small(i).start()

        @pl.loop(0, TILES)
        def _(t):
            for i in results:
                result(t, i).wait()

        for i in range(2):
            small(i).wait()


def chain(stage, base, meta, g, x, gain, weights, pm, qm, state):
    rows, width = g.shape
    depth = weights[0].shape[2]
    tokens = x.shape[0]
    side = 2 * BLOCK
    fresh = state is None
    off = 0 if stage == 0 else 1
    held = 0 if fresh else 3

    def kernel(*refs):
        ins, rest = refs[:8], refs[8 + held :]
        if stage == 0:
            rest = (None,) + rest
        chain_kernel(stage, base, *ins, *rest)

    out_shape = [
        jax.ShapeDtypeStruct((rows, width), BF16),
        pltpu.HBM((tokens, width), BF16),
        pltpu.HBM((tokens, side), F32),
        pltpu.HBM((tokens, side), F32),
    ][1 - off :]
    outs = pl.pallas_call(
        kernel,
        out_shape=out_shape,
        in_specs=[SMEM, ANY, ANY, VMEM, VMEM, VMEM, VMEM, VMEM] + [ANY] * held,
        out_specs=[ANY] * len(out_shape),
        input_output_aliases={8 + i: off + i for i in range(held)},
        scratch_shapes=[
            pltpu.VMEM((rows, width), BF16),
            pltpu.VMEM((rows, width), BF16),
            pltpu.VMEM((rows, width), F32),
            pltpu.VMEM((rows, width), BF16),
            pltpu.VMEM((rows, depth), F32),
            pltpu.VMEM((rows, depth), BF16),
            pltpu.VMEM((2, rows, side), F32),
            pltpu.SemaphoreType.DMA((5,)),
            pltpu.SemaphoreType.DMA((2, TILES)),
        ],
        compiler_params=pltpu.CompilerParams(vmem_limit_bytes=16 << 20),
        cost_estimate=pl.CostEstimate(
            flops=4 * rows * width * depth, bytes_accessed=10 * rows * width, transcendentals=0
        ),
        name=f"chain_{stage}_{base}",
    )(meta, g, x, *resident([gain, *weights, pm, qm]), *(() if fresh else outside(state)))
    if stage == 0:
        return None, tuple(outs)
    return outs[0], tuple(outs[1:])


def value_kernel(h, wv, qm, after, out, acc_s, out_s, sem):
    shards, depth = wv.shape[0], wv.shape[2]
    per = shards // TILES
    step = shards * wv.shape[1] // TILES
    acc_s[...] = jnp.zeros_like(acc_s)

    @pl.loop(0, TILES)
    def _(t):
        acc_s[...] += jnp.dot(
            h[:, pl.ds(pl.multiple_of(t * step, step), step)],
            wv[pl.ds(pl.multiple_of(t * per, per), per)].reshape(step, depth),
            preferred_element_type=F32,
        )

    out_s[...] = jnp.dot(acc_s[...].astype(BF16), qm[...], preferred_element_type=F32)
    copy = pltpu.make_async_copy(out_s, out, sem)
    copy.start()
    copy.wait()


def value_proj(h, wv, qm, after):
    rows, width = h.shape
    depth = wv.shape[2]
    return pl.pallas_call(
        value_kernel,
        out_shape=pltpu.HBM((rows, 2 * BLOCK), F32),
        in_specs=[VMEM, VMEM, VMEM, ANY],
        out_specs=ANY,
        scratch_shapes=[
            pltpu.VMEM((rows, depth), F32),
            pltpu.VMEM((rows, 2 * BLOCK), F32),
            pltpu.SemaphoreType.DMA,
        ],
        compiler_params=pltpu.CompilerParams(vmem_limit_bytes=16 << 20),
        cost_estimate=pl.CostEstimate(
            flops=2 * rows * width * depth, bytes_accessed=2 * rows * width, transcendentals=0
        ),
        name="value_proj",
    )(h, *resident([wv, qm]), after)


def score_kernel(
    first, docs, scale, meta, owners, lens, hp, vp, gp, dvp, panels, out,
    hp_s, vp_s, gp_s, dvp_s, panel_s, feat_s, acc_s, sem,
):
    slots = hp_s.shape[0] // docs
    side = hp.shape[1]
    dims = (((0,), (0,)), ((), ()))
    window = pl.ds(first * slots, docs * slots)
    loads = [
        pltpu.make_async_copy(src.at[window], dst, sem.at[i])
        for i, (src, dst) in enumerate(((hp, hp_s), (dvp, dvp_s), (gp, gp_s), (vp, vp_s)))
    ]
    whole = pltpu.make_async_copy(panels, panel_s, sem.at[4])
    for c in loads:
        c.start()
    whole.start()
    for c in loads:
        c.wait()
    for d in range(docs):
        rows = slice(d * slots, (d + 1) * slots)
        inv = scale / lens[first + d].astype(F32)
        for i, (a, b) in enumerate(((hp_s, dvp_s), (gp_s, vp_s))):
            f = lax.dot_general(
                a[rows, :], b[rows, :], dims, precision=lax.Precision.HIGHEST,
                preferred_element_type=F32,
            )
            feat_s[d, i * side : (i + 1) * side, :] = (f * inv).astype(BF16).astype(F32)

    whole.wait()

    def item(j, carry):
        owner = owners[j]
        far = lax.rem(owner + SIDE - meta[3], SIDE)
        p = panel_s[owner // SIDE, far].astype(F32)
        for d in range(docs):
            acc_s[d, pl.ds(j, 1), :] = jnp.sum(p * feat_s[d], axis=0, keepdims=True)
        return carry

    lax.fori_loop(0, owners.shape[0], item, 0)
    ones = jnp.ones((8, side), F32)
    for d in range(docs):
        total = lax.dot_general(
            ones, acc_s[d], (((1,), (1,)), ((), ())), precision=lax.Precision.HIGHEST,
            preferred_element_type=F32,
        )
        out[d : d + 1, :] = total[:1] * (1.0 / side)


def score(first, docs, meta, owners, lens, hp, vp, gp, dvp, panels):
    items = owners.shape[0]
    high, side = panels.shape[2:]
    rows = hp.shape[0] // lens.shape[0] * docs
    return pl.pallas_call(
        functools.partial(score_kernel, first, docs, 1.0 / 16),
        out_shape=jax.ShapeDtypeStruct((docs, items), F32),
        in_specs=[SMEM, SMEM, SMEM] + [ANY] * 5,
        out_specs=VMEM,
        scratch_shapes=[pltpu.VMEM((rows, side), F32)] * 4
        + [
            pltpu.VMEM(panels.shape, BF16),
            pltpu.VMEM((docs, high, side), F32),
            pltpu.VMEM((docs, items, side), F32),
            pltpu.SemaphoreType.DMA((5,)),
        ],
        compiler_params=pltpu.CompilerParams(vmem_limit_bytes=12 << 20),
        name=f"score_{first}",
    )(meta, owners, lens, *outside([hp, vp, gp, dvp, panels]))


def index_of(coord):
    return (coord[0] * SIDE + coord[1]) * SIDE + coord[2]


def fetch(block, axis, distance):
    route = []
    for i in range(SIDE**3):
        coord = [i // SIDE**2, i // SIDE % SIDE, i % SIDE]
        coord[axis] = (coord[axis] + distance) % SIDE
        route.append((index_of(coord), i))
    return lax.ppermute(block, "dp", route)


def plane(block):
    groups = [
        [index_of((x, y, z)) for x in range(SIDE) for y in range(SIDE)] for z in range(SIDE)
    ]
    return lax.all_gather(block, "dp", axis=0, tiled=True, axis_index_groups=groups)


def two_axes(blocks):
    axes = ((0, 1), (1, 0))
    near = [[fetch(k, p, d) for d in (1, -1, 2)] for k, (p, _) in zip(blocks, axes)]
    near = lax.optimization_barrier(near)
    half = SIDE // 2
    low = [jnp.stack([k, up]) for k, (up, _, _) in zip(blocks, near)]
    high = [jnp.stack([far, down]) for _, down, far in near]
    up_low = [fetch(k, q, 1) for k, (_, q) in zip(low, axes)]
    down_high = [fetch(k, q, -1) for k, (_, q) in zip(high, axes)]
    low, high, up_low, down_high = lax.optimization_barrier((low, high, up_low, down_high))
    up_high = [fetch(k, q, 1) for k, (_, q) in zip(high, axes)]
    down_low = [fetch(k, q, -1) for k, (_, q) in zip(low, axes)]
    far_low = [fetch(k, q, 1) for k, (_, q) in zip(up_low, axes)]
    far_high = [fetch(k, q, -1) for k, (_, q) in zip(down_high, axes)]
    early = [(low, 0, 0), (high, half, 0), (up_low, 0, 1), (down_high, half, SIDE - 1)]
    late = [(up_high, half, 1), (down_low, 0, SIDE - 1), (far_low, 0, 2), (far_high, half, 2)]
    return [
        (
            [(kind, axes[kind], fixed, start) for _, start, fixed in group for kind in range(2)],
            [got[kind] for got, _, _ in group for kind in range(2)],
        )
        for group in (early, late)
    ]


def body(acts, cotangent, gains, value_w, output_w, d_map, r_map, lengths, item_panels, owners):
    sections = lax.axis_size("section")
    section = lax.axis_index("section")
    place = lax.axis_index("dp")
    meta = jnp.stack([section, place // SIDE**2, place // SIDE % SIDE, place % SIDE])
    x = acts[0]
    tokens, width = x.shape
    docs = lengths.shape[0]
    slots = tokens // docs
    per, depth = value_w.shape[1:]

    own = jnp.stack([value_w[0], output_w[0].T])
    own_plane = plane(own[None])
    panel = item_panels.reshape(-1, 2 * BLOCK)
    flat = jnp.concatenate([own.reshape(-1, depth), panel.reshape(-1, depth)])
    others = [fetch(flat, 2, d) for d in range(1, SIDE)]
    pm, qm, hidden, hp = prepare(d_map, r_map, x, gains)
    live = (jnp.arange(slots, dtype=jnp.int32)[None, :] < lengths[:, None]).reshape(docs, slots, 1)
    cot = jnp.where(live, cotangent.reshape(docs, slots, width), 0).astype(BF16)
    cot = cot.reshape(tokens, width)
    rows = tokens // CHUNKS
    incoming = [cot[c * rows : (c + 1) * rows] for c in range(CHUNKS)]
    others, pm, hidden, incoming = lax.optimization_barrier((others, pm, hidden, incoming))
    others = jnp.stack(others)
    early, late = two_axes((others[:, :per], others[:, per : 2 * per]))
    panels = jnp.concatenate([panel[None], others[:, 2 * per :].reshape(SIDE - 1, -1, 2 * BLOCK)])
    panels, late[1][:] = lax.optimization_barrier((panels, late[1]))
    panels = plane(panels[None])

    shape = (SIDE**3, per, depth)
    weights = load([(None,) * 4] + early[0], meta, [own_plane] + early[1], None, shape)
    weights = load(late[0], meta, late[1], weights, shape)

    state = vp = None
    for stage in range(sections - 1, -1, -1):
        arrived = []
        for c in range(CHUNKS):
            send, state = chain(
                stage, c * rows, meta, incoming[c], x, gains, weights, pm, qm, state
            )
            if stage > 0:
                arrived.append(lax.ppermute(send, "section", [(stage, stage - 1)]))
        incoming = arrived
        if vp is None:
            vp = value_proj(hidden, weights[0], qm, send)
    grads = state[0]
    part = score(0, docs, meta, owners, lengths, hp, vp, *state[1:], panels)
    total = part
    for k in range(1, sections):
        total = total + lax.ppermute(
            part, "section", [(i, (i + k) % sections) for i in range(sections)]
        )
    return (grads[None], total)


def solution(mesh):
    in_specs = (
        P("section", "dp", None),
        P("dp", None),
        P("section", None),
        P("section", "dp", None),
        P("section", None, "dp"),
        P("section", None),
        P("section", None),
        P("dp"),
        P("dp", "section", None, None, None),
        P(),
    )
    out_specs = (P("section", "dp", None), P("dp", None))
    return jax.shard_map(body, mesh=mesh, in_specs=in_specs, out_specs=out_specs, check_vma=False)
```

```python
import functools

import jax
import jax.numpy as jnp
from jax import lax
from jax.experimental import pallas as pl
from jax.experimental.pallas import tpu as pltpu
from jax.sharding import PartitionSpec as P

BLOCK = 64
EPS = 1e-05
ANY = pl.BlockSpec(memory_space=pl.ANY)
SMEM = pl.BlockSpec(memory_space=pltpu.SMEM)
VMEM = pl.BlockSpec(memory_space=pltpu.VMEM)
F32 = jnp.float32
BF16 = jnp.bfloat16
TILES = 8
FINE = 256
CHUNKS = 3
SIDE = 4


def prepare_kernel(d_map, r_map, x, gain, pm, qm, hidden, hp, hp_s, sem):
    row = lax.broadcasted_iota(jnp.int32, (BLOCK, 2 * BLOCK), 0)
    col = lax.broadcasted_iota(jnp.int32, (BLOCK, 2 * BLOCK), 1)
    unit = [jnp.where(row + k * BLOCK == col, 1.0, 0.0).astype(F32) for k in range(2)]
    for codes, out in ((d_map, pm), (r_map, qm)):

        @pl.loop(0, codes.shape[1])
        def _(b, codes=codes, out=out):
            code = codes[0, b]
            sign = (1 - 2 * (code // 2)).astype(F32)
            high = (code % 2).astype(F32)
            block = sign * (unit[0] * (1.0 - high) + unit[1] * high)
            out[pl.ds(pl.multiple_of(b * BLOCK, BLOCK), BLOCK), :] = block.astype(BF16)

    part = 128

    @pl.loop(0, x.shape[0] // part)
    def _(i):
        at = pl.ds(pl.multiple_of(i * part, part), part)
        xf = x[at, :].astype(F32)
        r = lax.rsqrt(jnp.mean(xf * xf, axis=-1, keepdims=True) + EPS)
        hidden[at, :] = (xf * r * gain[...]).astype(BF16)
        hp_s[at, :] = jnp.dot(hidden[at, :], pm[...], preferred_element_type=F32)

    copy = pltpu.make_async_copy(hp_s, hp, sem)
    copy.start()
    copy.wait()


def prepare(d_map, r_map, x, gain):
    rows, width = x.shape
    depth = r_map.shape[1] * BLOCK
    side = 2 * BLOCK
    return pl.pallas_call(
        prepare_kernel,
        out_shape=[
            pltpu.VMEM((width, side), BF16),
            pltpu.VMEM((depth, side), BF16),
            jax.ShapeDtypeStruct((rows, width), BF16),
            pltpu.HBM((rows, side), F32),
        ],
        in_specs=[SMEM, SMEM, VMEM, VMEM],
        out_specs=[VMEM] * 3 + [ANY],
        scratch_shapes=[pltpu.VMEM((rows, side), F32), pltpu.SemaphoreType.DMA],
        compiler_params=pltpu.CompilerParams(vmem_limit_bytes=24 << 20),
        cost_estimate=pl.CostEstimate(
            flops=4 * rows * width * side, bytes_accessed=6 * rows * width, transcendentals=0
        ),
        name="prepare",
    )(d_map, r_map, x, gain)


def load_kernel(plan, first, *refs):
    meta = refs[0]
    pieces = refs[1 : 1 + len(plan)]
    n = 1 + len(plan) + (0 if first else 2)
    outs = refs[n : n + 2]
    sem = refs[n + 2]
    me = (meta[1], meta[2], meta[3])

    def place(coord):
        return (coord[0] * SIDE + coord[1]) * SIDE + coord[2]

    def copies(go):
        at = 0
        for ref, (kind, axes, fixed, start) in zip(pieces, plan):
            if kind is None:
                count = ref.shape[0] * 2

                def one(i, ref=ref, at=at):
                    for k in range(2):
                        yield ref.at[i, k], outs[k].at[i * SIDE + me[2]], sem.at[at + 2 * i + k]

                total = ref.shape[0]
            else:
                p, q = axes
                deep = ref.shape[1]
                count = ref.shape[0] * deep

                def one(i, ref=ref, at=at, kind=kind, p=p, q=q, fixed=fixed, start=start, deep=deep):
                    near, far = i // deep, i % deep
                    coord = [None, None, (me[2] + 1 + far) % SIDE]
                    coord[p] = (me[p] + start + near) % SIDE
                    coord[q] = (me[q] + fixed) % SIDE
                    yield ref.at[near, far], outs[kind].at[place(coord)], sem.at[at + i]

                total = count

            @pl.loop(0, total)
            def _(i, one=one):
                for src, dst, sm in one(i):
                    go(pltpu.make_async_copy(src, dst, sm))

            at += count

    copies(lambda c: c.start())
    copies(lambda c: c.wait())


def outside(arrays):
    return [pltpu.with_memory_space_constraint(w, pltpu.HBM) for w in arrays]


def resident(weights):
    return [pltpu.with_memory_space_constraint(w, pltpu.VMEM) for w in weights]


def load(plan, meta, pieces, weights, shape):
    first = weights is None
    count = sum(p.shape[0] * p.shape[1] for p in pieces)
    n = 1 + len(pieces)
    return pl.pallas_call(
        functools.partial(load_kernel, plan, first),
        out_shape=[pltpu.VMEM(shape, BF16)] * 2,
        in_specs=[SMEM] + [ANY] * len(pieces) + ([] if first else [VMEM] * 2),
        out_specs=[VMEM] * 2,
        input_output_aliases={} if first else {n: 0, n + 1: 1},
        scratch_shapes=[pltpu.SemaphoreType.DMA((count,))],
        compiler_params=pltpu.CompilerParams(vmem_limit_bytes=4 << 20),
        cost_estimate=pl.CostEstimate(
            flops=0, bytes_accessed=sum(p.size for p in pieces) * 2, transcendentals=0
        ),
        name="load_first" if first else "load_last",
    )(meta, *outside(pieces), *(() if first else resident(weights)))


def chain_kernel(
    stage, base, meta, g_hbm, x_hbm, gain, wv, wo, pm, qm, send, grads, gp, dvp,
    g_s, x_s, u_s, out_s, acc_s, dv_s, p_s, in_sem, out_sem,
):
    rows, width = g_s.shape
    shards, depth = wo.shape[0], wo.shape[2]
    per = shards // TILES
    step = width // TILES

    def weight(ref, t):
        return ref[pl.ds(pl.multiple_of(t * per, per), per)].reshape(step, depth)

    def columns(t, size=step):
        return pl.ds(pl.multiple_of(t * size, size), size)

    def result(t, i):
        at = columns(t, FINE)
        dst = grads.at[pl.ds(base, rows), at] if i == 0 else send.at[:, at]
        return pltpu.make_async_copy(out_s.at[:, at], dst, out_sem.at[i, t])

    def small(i):
        dst = (gp, dvp)[i].at[pl.ds(base, rows)]
        return pltpu.make_async_copy(p_s.at[i], dst, in_sem.at[3 + i])

    results = range(1 if send is None else 2)

    @pl.when(meta[0] == stage)
    def _():
        cg = pltpu.make_async_copy(g_hbm, g_s, in_sem.at[0])
        cx = pltpu.make_async_copy(x_hbm.at[pl.ds(base, rows)], x_s, in_sem.at[1])
        cg.start()
        cx.start()
        acc_s[...] = jnp.zeros_like(acc_s)
        cg.wait()

        @pl.loop(0, TILES)
        def _(t):
            acc_s[...] += jnp.dot(g_s[:, columns(t)], weight(wo, t), preferred_element_type=F32)

        dv_s[...] = acc_s[...].astype(BF16)
        cx.wait()

        def back(t, sums):
            dh = lax.dot_general(
                dv_s[...], weight(wv, t), (((1,), (1,)), ((), ())), preferred_element_type=F32
            )
            at = columns(t)
            u = dh * gain[:, at]
            x = x_s[:, at].astype(F32)
            u_s[:, at] = u
            return (
                sums[0] + jnp.sum(u * x, axis=-1, keepdims=True),
                sums[1] + jnp.sum(x * x, axis=-1, keepdims=True),
            )

        zero = jnp.zeros((rows, 1), F32)
        total, square = lax.fori_loop(0, TILES, back, (zero, zero))
        r = lax.rsqrt(square * (1.0 / width) + EPS)
        drop = r * r * r * total * (1.0 / width)

        @pl.loop(0, width // FINE)
        def _(t):
            at = columns(t, FINE)
            grad = g_s[:, at].astype(F32) + (r * u_s[:, at] - drop * x_s[:, at].astype(F32))
            out_s[:, at] = grad.astype(BF16)
            for i in results:
                result(t, i).start()

        p_s[0] = jnp.zeros_like(p_s[0])

        @pl.loop(0, TILES)
        def _(t):
            p_s[0] += jnp.dot(g_s[:, columns(t)], pm[columns(t), :], preferred_element_type=F32)

        p_s[1] = jnp.dot(dv_s[...], qm[...], preferred_element_type=F32)
        for i in range(2):
            small(i).start()

        @pl.loop(0, width // FINE)
        def _(t):
            for i in results:
                result(t, i).wait()

        for i in range(2):
            small(i).wait()


def chain(stage, base, meta, g, x, gain, weights, pm, qm, state):
    rows, width = g.shape
    depth = weights[0].shape[2]
    tokens = x.shape[0]
    side = 2 * BLOCK
    fresh = state is None
    off = 0 if stage == 0 else 1
    held = 0 if fresh else 3

    def kernel(*refs):
        ins, rest = refs[:8], refs[8 + held :]
        if stage == 0:
            rest = (None,) + rest
        chain_kernel(stage, base, *ins, *rest)

    out_shape = [
        jax.ShapeDtypeStruct((rows, width), BF16),
        pltpu.HBM((tokens, width), BF16),
        pltpu.HBM((tokens, side), F32),
        pltpu.HBM((tokens, side), F32),
    ][1 - off :]
    outs = pl.pallas_call(
        kernel,
        out_shape=out_shape,
        in_specs=[SMEM, ANY, ANY, VMEM, VMEM, VMEM, VMEM, VMEM] + [ANY] * held,
        out_specs=[ANY] * len(out_shape),
        input_output_aliases={8 + i: off + i for i in range(held)},
        scratch_shapes=[
            pltpu.VMEM((rows, width), BF16),
            pltpu.VMEM((rows, width), BF16),
            pltpu.VMEM((rows, width), F32),
            pltpu.VMEM((rows, width), BF16),
            pltpu.VMEM((rows, depth), F32),
            pltpu.VMEM((rows, depth), BF16),
            pltpu.VMEM((2, rows, side), F32),
            pltpu.SemaphoreType.DMA((5,)),
            pltpu.SemaphoreType.DMA((2, width // FINE)),
        ],
        compiler_params=pltpu.CompilerParams(vmem_limit_bytes=16 << 20),
        cost_estimate=pl.CostEstimate(
            flops=4 * rows * width * depth, bytes_accessed=10 * rows * width, transcendentals=0
        ),
        name=f"chain_{stage}_{base}",
    )(meta, g, x, *resident([gain, *weights, pm, qm]), *(() if fresh else outside(state)))
    if stage == 0:
        return None, tuple(outs)
    return outs[0], tuple(outs[1:])


def value_kernel(h, wv, qm, after, out, acc_s, out_s, sem):
    shards, depth = wv.shape[0], wv.shape[2]
    per = shards // TILES
    step = shards * wv.shape[1] // TILES
    acc_s[...] = jnp.zeros_like(acc_s)

    @pl.loop(0, TILES)
    def _(t):
        acc_s[...] += jnp.dot(
            h[:, pl.ds(pl.multiple_of(t * step, step), step)],
            wv[pl.ds(pl.multiple_of(t * per, per), per)].reshape(step, depth),
            preferred_element_type=F32,
        )

    out_s[...] = jnp.dot(acc_s[...].astype(BF16), qm[...], preferred_element_type=F32)
    copy = pltpu.make_async_copy(out_s, out, sem)
    copy.start()
    copy.wait()


def value_proj(h, wv, qm, after):
    rows, width = h.shape
    depth = wv.shape[2]
    return pl.pallas_call(
        value_kernel,
        out_shape=pltpu.HBM((rows, 2 * BLOCK), F32),
        in_specs=[VMEM, VMEM, VMEM, ANY],
        out_specs=ANY,
        scratch_shapes=[
            pltpu.VMEM((rows, depth), F32),
            pltpu.VMEM((rows, 2 * BLOCK), F32),
            pltpu.SemaphoreType.DMA,
        ],
        compiler_params=pltpu.CompilerParams(vmem_limit_bytes=16 << 20),
        cost_estimate=pl.CostEstimate(
            flops=2 * rows * width * depth, bytes_accessed=2 * rows * width, transcendentals=0
        ),
        name="value_proj",
    )(h, *resident([wv, qm]), after)


def score_kernel(
    first, docs, scale, meta, owners, lens, hp, vp, gp, dvp, panels, out,
    hp_s, vp_s, gp_s, dvp_s, panel_s, feat_s, acc_s, sem,
):
    slots = hp_s.shape[0] // docs
    side = hp.shape[1]
    dims = (((0,), (0,)), ((), ()))
    window = pl.ds(first * slots, docs * slots)
    loads = [
        pltpu.make_async_copy(src.at[window], dst, sem.at[i])
        for i, (src, dst) in enumerate(((hp, hp_s), (dvp, dvp_s), (gp, gp_s), (vp, vp_s)))
    ]
    whole = pltpu.make_async_copy(panels, panel_s, sem.at[4])
    for c in loads:
        c.start()
    whole.start()
    for c in loads:
        c.wait()
    for d in range(docs):
        rows = slice(d * slots, (d + 1) * slots)
        inv = scale / lens[first + d].astype(F32)
        for i, (a, b) in enumerate(((hp_s, dvp_s), (gp_s, vp_s))):
            f = lax.dot_general(
                a[rows, :], b[rows, :], dims, precision=lax.Precision.HIGHEST,
                preferred_element_type=F32,
            )
            feat_s[d, i * side : (i + 1) * side, :] = (f * inv).astype(BF16).astype(F32)

    whole.wait()

    def item(j, carry):
        owner = owners[j]
        far = lax.rem(owner + SIDE - meta[3], SIDE)
        p = panel_s[owner // SIDE, far].astype(F32)
        for d in range(docs):
            acc_s[d, pl.ds(j, 1), :] = jnp.sum(p * feat_s[d], axis=0, keepdims=True)
        return carry

    lax.fori_loop(0, owners.shape[0], item, 0)
    ones = jnp.ones((8, side), F32)
    for d in range(docs):
        total = lax.dot_general(
            ones, acc_s[d], (((1,), (1,)), ((), ())), precision=lax.Precision.HIGHEST,
            preferred_element_type=F32,
        )
        out[d : d + 1, :] = total[:1] * (1.0 / side)


def score(first, docs, meta, owners, lens, hp, vp, gp, dvp, panels):
    items = owners.shape[0]
    high, side = panels.shape[2:]
    rows = hp.shape[0] // lens.shape[0] * docs
    return pl.pallas_call(
        functools.partial(score_kernel, first, docs, 1.0 / 16),
        out_shape=jax.ShapeDtypeStruct((docs, items), F32),
        in_specs=[SMEM, SMEM, SMEM] + [ANY] * 5,
        out_specs=VMEM,
        scratch_shapes=[pltpu.VMEM((rows, side), F32)] * 4
        + [
            pltpu.VMEM(panels.shape, BF16),
            pltpu.VMEM((docs, high, side), F32),
            pltpu.VMEM((docs, items, side), F32),
            pltpu.SemaphoreType.DMA((5,)),
        ],
        compiler_params=pltpu.CompilerParams(vmem_limit_bytes=12 << 20),
        name=f"score_{first}",
    )(meta, owners, lens, *outside([hp, vp, gp, dvp, panels]))


def index_of(coord):
    return (coord[0] * SIDE + coord[1]) * SIDE + coord[2]


def fetch(block, axis, distance):
    route = []
    for i in range(SIDE**3):
        coord = [i // SIDE**2, i // SIDE % SIDE, i % SIDE]
        coord[axis] = (coord[axis] + distance) % SIDE
        route.append((index_of(coord), i))
    return lax.ppermute(block, "dp", route)


def plane(block):
    groups = [
        [index_of((x, y, z)) for x in range(SIDE) for y in range(SIDE)] for z in range(SIDE)
    ]
    return lax.all_gather(block, "dp", axis=0, tiled=True, axis_index_groups=groups)


def two_axes(blocks):
    axes = ((0, 1), (1, 0))
    near = [[fetch(k, p, d) for d in (1, -1, 2)] for k, (p, _) in zip(blocks, axes)]
    near = lax.optimization_barrier(near)
    half = SIDE // 2
    low = [jnp.stack([k, up]) for k, (up, _, _) in zip(blocks, near)]
    high = [jnp.stack([far, down]) for _, down, far in near]
    up_low = [fetch(k, q, 1) for k, (_, q) in zip(low, axes)]
    down_high = [fetch(k, q, -1) for k, (_, q) in zip(high, axes)]
    low, high, up_low, down_high = lax.optimization_barrier((low, high, up_low, down_high))
    up_high = [fetch(k, q, 1) for k, (_, q) in zip(high, axes)]
    down_low = [fetch(k, q, -1) for k, (_, q) in zip(low, axes)]
    far_low = [fetch(k, q, 1) for k, (_, q) in zip(up_low, axes)]
    far_high = [fetch(k, q, -1) for k, (_, q) in zip(down_high, axes)]
    early = [(low, 0, 0), (high, half, 0), (up_low, 0, 1), (down_high, half, SIDE - 1)]
    late = [(up_high, half, 1), (down_low, 0, SIDE - 1), (far_low, 0, 2), (far_high, half, 2)]
    return [
        (
            [(kind, axes[kind], fixed, start) for _, start, fixed in group for kind in range(2)],
            [got[kind] for got, _, _ in group for kind in range(2)],
        )
        for group in (early, late)
    ]


def body(acts, cotangent, gains, value_w, output_w, d_map, r_map, lengths, item_panels, owners):
    sections = lax.axis_size("section")
    section = lax.axis_index("section")
    place = lax.axis_index("dp")
    meta = jnp.stack([section, place // SIDE**2, place // SIDE % SIDE, place % SIDE])
    x = acts[0]
    tokens, width = x.shape
    docs = lengths.shape[0]
    slots = tokens // docs
    per, depth = value_w.shape[1:]

    own = jnp.stack([value_w[0], output_w[0].T])
    own_plane = plane(own[None])
    panel = item_panels.reshape(-1, 2 * BLOCK)
    flat = jnp.concatenate([own.reshape(-1, depth), panel.reshape(-1, depth)])
    others = [fetch(flat, 2, d) for d in range(1, SIDE)]
    pm, qm, hidden, hp = prepare(d_map, r_map, x, gains)
    live = (jnp.arange(slots, dtype=jnp.int32)[None, :] < lengths[:, None]).reshape(docs, slots, 1)
    cot = jnp.where(live, cotangent.reshape(docs, slots, width), 0).astype(BF16)
    cot = cot.reshape(tokens, width)
    rows = tokens // CHUNKS
    incoming = [cot[c * rows : (c + 1) * rows] for c in range(CHUNKS)]
    others, pm, hidden, incoming = lax.optimization_barrier((others, pm, hidden, incoming))
    others = jnp.stack(others)
    early, late = two_axes((others[:, :per], others[:, per : 2 * per]))
    panels = jnp.concatenate([panel[None], others[:, 2 * per :].reshape(SIDE - 1, -1, 2 * BLOCK)])
    panels, late[1][:] = lax.optimization_barrier((panels, late[1]))
    panels = plane(panels[None])

    shape = (SIDE**3, per, depth)
    weights = load([(None,) * 4] + early[0], meta, [own_plane] + early[1], None, shape)
    weights = load(late[0], meta, late[1], weights, shape)

    state = vp = None
    for stage in range(sections - 1, -1, -1):
        arrived = []
        for c in range(CHUNKS):
            send, state = chain(
                stage, c * rows, meta, incoming[c], x, gains, weights, pm, qm, state
            )
            if stage > 0:
                arrived.append(lax.ppermute(send, "section", [(stage, stage - 1)]))
        incoming = arrived
        if vp is None:
            vp = value_proj(hidden, weights[0], qm, send)
    grads = state[0]
    part = score(0, docs, meta, owners, lengths, hp, vp, *state[1:], panels)
    total = part
    for k in range(1, sections):
        total = total + lax.ppermute(
            part, "section", [(i, (i + k) % sections) for i in range(sections)]
        )
    return (grads[None], total)


def solution(mesh):
    in_specs = (
        P("section", "dp", None),
        P("dp", None),
        P("section", None),
        P("section", "dp", None),
        P("section", None, "dp"),
        P("section", None),
        P("section", None),
        P("dp"),
        P("dp", "section", None, None, None),
        P(),
    )
    out_specs = (P("section", "dp", None), P("dp", None))
    return jax.shard_map(body, mesh=mesh, in_specs=in_specs, out_specs=out_specs, check_vma=False)
```
